32 devices in a mesh: query: 8 (over z, y), tensor: 2 (over x), dp: 2 (over core).
Axes of the slice: x: 2, y: 2, z: 4, core: 2. Of those that a mesh axis runs over, the one named last changes fastest.
Arguments:
- hidden: bfloat16 [16, 1024, 14336], P(('query', 'dp'), None, 'tensor'), may hold values from -6 to 6
- out_grad: bfloat16 [16, 1024, 4096], P(('query', 'dp'), None, 'tensor'), may hold values from -6 to 6
- proj_in: bfloat16 [14336, 64], P('tensor'), may hold values from -0.046875 to 0.046875
- proj_out: bfloat16 [4096, 64], P('tensor'), may hold values from -0.09375 to 0.09375
- seg_ids: int32 [16, 1024], P(('query', 'dp')), may hold values from 0 to 31, never falling along the last dimension, each value on 1 to 288 neighbouring positions
- queries: bfloat16 [1024, 4096], P(('query', 'dp'), 'tensor'), may hold values from -0.01171875 to 0.01171875
Outputs:
- scores: float32 [512, 1024], P('tensor', ('query', 'dp'))
The draws below stay inside these ranges and needn't reach their ends.
All inputs are finite; a program needn't handle non-finite values.
Results may differ from the reference program's by a relative error of at most 0.004.
Values may be sent and summed in bfloat16 or wider, within the bound.
No kernel may reach another device: no remote copies, remote signals or barrier semaphores. Data moves between devices by JAX's collectives and lax.ppermute only.
A program may use at most 64 MiB of HBM per device.

```python
import math
import jax
import jax.numpy as jnp
import numpy as np
from jax import lax

D = 4096
FF = 14336
K = 64
KK = 4096
LEN = 1024
SEGS = 32
ROWS = 16
NQ = 1024


def block_levels(own_key, shape, cuts, smallest, largest):
    gain, own = 1.0, jax.random.fold_in(own_key, 6)
    for dim, blocks in cuts:
        steps = jnp.exp(jax.random.uniform(jax.random.fold_in(own, dim), (blocks,), jnp.float32, smallest / len(cuts), largest / len(cuts)))
        gain = gain * jnp.repeat(steps, shape[dim] // blocks).reshape([-1 if axis == dim else 1 for axis in range(len(shape))])
    return gain


def split_up(amount, total, reach, lean):
    loads = [(1 << 20) // math.isqrt(grade ** lean) + 1 for grade in range(2, amount + 1)]
    surplus, counts = total - reach - (amount - 1), [1] * (amount - 1)
    while surplus > 0:
        candidates = [i for i in range(amount - 1) if counts[i] < reach]
        mass, left = sum([loads[i] for i in candidates]), surplus
        for i in candidates:
            addition = min(reach - counts[i], max(1, left * loads[i] // mass), surplus)
            counts[i] = counts[i] + addition
            surplus = surplus - addition
    return np.array([reach] + counts)


def uneven(stream_key, amount, total, limit, slope):
    if amount == 2:
        one = jax.random.randint(stream_key, (), max(1, total - limit), min(limit, total - 1) + 1)
        return jnp.stack([one, total - one])
    lengths = jnp.asarray(split_up(amount, total, limit, slope), jnp.int32)
    pairs = (amount - 1) // 2
    donor, receiver = lengths[1:1 + 2 * pairs:2], lengths[2:2 + 2 * pairs:2]
    slack = jnp.minimum(donor - 1, limit - receiver)
    moved = jax.random.randint(jax.random.fold_in(stream_key, 1), (pairs,), 0, 1 << 20) % (slack + 1)
    lengths = lengths.at[1:1 + 2 * pairs:2].set(donor - moved).at[2:2 + 2 * pairs:2].set(receiver + moved)
    return lengths[jax.random.permutation(jax.random.fold_in(stream_key, 2), amount)]


def gaussian(key, dims, scale, reach, pieces=(), held_as=jnp.bfloat16):
    factor_of = block_levels(key, dims, pieces, -0.22, 0.18) if pieces else 1.0
    drawn = jax.random.normal(key, dims, jnp.float32) * scale * factor_of
    return jnp.minimum(jnp.maximum(drawn, -reach), reach).astype(held_as)


def setup_inputs(seed: int = 0) -> dict:
    streams_of = jax.random.split(jax.random.key(seed), 7)
    hidden = gaussian(streams_of[0], (ROWS, LEN, FF), 1.0, 6.0, ((0, 16), (2, 2)))
    out_grad = gaussian(streams_of[1], (ROWS, LEN, D), 1.0, 6.0, ((0, 16), (2, 2)))
    proj_in = gaussian(streams_of[2], (FF, K), FF ** -0.5, 0.046875, ((0, 2),))
    proj_out = gaussian(streams_of[3], (D, K), D ** -0.5, 0.09375, ((0, 2),))
    seg_ids = jax.vmap(lambda own: jnp.searchsorted(jnp.cumsum(uneven(own, SEGS, LEN, LEN // 4 + 32, 2)), jnp.arange(LEN), side="right"))(jax.random.split(streams_of[4], ROWS)).reshape((ROWS, LEN)).astype(jnp.int32)
    queries = gaussian(streams_of[5], (NQ, KK), (64 * KK) ** -0.5, 0.01171875, ((0, 16), (1, 2)))
    return {"hidden": hidden, "out_grad": out_grad, "proj_in": proj_in, "proj_out": proj_out, "seg_ids": seg_ids, "queries": queries}


def row_features(hidden_row, grad_row, seg_row, proj_in, proj_out):
    act_proj = jnp.dot(hidden_row, proj_in, preferred_element_type=jnp.float32)
    grad_proj = jnp.dot(grad_row, proj_out, preferred_element_type=jnp.float32)
    outer = (grad_proj[:, :, None] * act_proj[:, None, :]).reshape(hidden_row.shape[0], -1).astype(jnp.bfloat16)
    member = (seg_row[None, :] == jnp.arange(SEGS, dtype=jnp.int32)[:, None]).astype(jnp.bfloat16)
    return jnp.dot(member, outer, preferred_element_type=jnp.float32).astype(jnp.bfloat16)


def reference(hidden, out_grad, proj_in, proj_out, seg_ids, queries):
    feats = lax.map(lambda item: row_features(item[0], item[1], item[2], proj_in, proj_out), (hidden, out_grad, seg_ids))
    doc_feats = feats.reshape(ROWS * SEGS, KK)
    return lax.dot_general(doc_feats, queries, (((1,), (1,)), ((), ())), preferred_element_type=jnp.float32)
```

```python
import functools
import math

import jax
import jax.numpy as jnp
from jax import lax
from jax.experimental import pallas as pl
from jax.experimental.pallas import tpu as pltpu
from jax.sharding import PartitionSpec as P

SEGS = 32
MIB = 2**20
NT = (((1,), (1,)), ((), ()))
VMEM = pl.BlockSpec(memory_space=pltpu.VMEM)
SMEM = pl.BlockSpec(memory_space=pltpu.SMEM)
ANY = pl.BlockSpec(memory_space=pl.ANY)


def tiles(length, tile):
    return [(start, min(tile, length - start)) for start in range(0, length, tile)]


def project_kernel(parts, place, hidden, grads, w_in, w_out, keep, send, h_buf, g_buf, wi_buf, wo_buf, out_side, h_sem, g_sem, w_sem):
    length, width = h_buf.shape[0], w_in.shape[0]
    block = width // parts
    weights = [pltpu.make_async_copy(w_out, wo_buf, w_sem.at[0]), pltpu.make_async_copy(w_in, wi_buf, w_sem.at[1])]
    spans = tiles(length, 256)
    weights[0].start()
    copies = []
    for n, (start, size) in enumerate(spans):
        rows = pl.ds(start, size)
        copies.append(
            (
                pltpu.make_async_copy(grads.at[rows], g_buf.at[rows], g_sem.at[n]),
                pltpu.make_async_copy(hidden.at[rows], h_buf.at[rows], h_sem.at[n]),
            )
        )
    copies[0][0].start()
    weights[1].start()
    copies[0][1].start()
    for first, second in copies[1:]:
        first.start()
        second.start()
    for n, (start, size) in enumerate(spans):
        rows = slice(start, start + size)
        if n == 0:
            weights[0].wait()
        copies[n][0].wait()
        out_side[:, rows] = lax.dot_general(wo_buf[...], g_buf[rows], NT, preferred_element_type=jnp.float32)
        if n == 0:
            weights[1].wait()
        copies[n][1].wait()
        act = lax.dot_general(wi_buf[...], h_buf[rows], NT, preferred_element_type=jnp.float32)
        keep[:width, rows] = act
        for d in range(1, parts):
            send[d - 1, :width, rows] = act.astype(jnp.bfloat16)
    keep[width:] = out_side[pl.ds(pl.multiple_of(place[0] * block, block), block)]
    for d in range(1, parts):
        there = lax.rem(place[0] + d, parts)
        send[d - 1, width:] = out_side[pl.ds(pl.multiple_of(there * block, block), block)].astype(jnp.bfloat16)


def project(parts, place, hidden, grads, w_in, w_out):
    (length, units), features, width = hidden.shape, grads.shape[1], w_in.shape[0]
    rows, steps = width + width // parts, len(tiles(length, 256))
    return pl.pallas_call(
        functools.partial(project_kernel, parts),
        out_shape=(
            jax.ShapeDtypeStruct((rows, length), jnp.float32),
            jax.ShapeDtypeStruct((max(parts - 1, 1), rows, length), jnp.bfloat16),
        ),
        in_specs=[SMEM, ANY, ANY, ANY, ANY],
        out_specs=(VMEM, VMEM),
        scratch_shapes=[
            pltpu.VMEM((length, units), jnp.bfloat16),
            pltpu.VMEM((length, features), jnp.bfloat16),
            pltpu.VMEM((width, units), jnp.bfloat16),
            pltpu.VMEM((width, features), jnp.bfloat16),
            pltpu.VMEM((width, length), jnp.float32),
            pltpu.SemaphoreType.DMA((steps,)),
            pltpu.SemaphoreType.DMA((steps,)),
            pltpu.SemaphoreType.DMA((2,)),
        ],
        compiler_params=pltpu.CompilerParams(vmem_limit_bytes=40 * MIB),
        name="project",
    )(place, hidden, grads, w_in, w_out)


def features_kernel(width, segment, keep, *rest):
    received, out = rest[:-1], rest[-1]
    total = keep[...]
    for other in received:
        total = total + other[...].astype(jnp.float32)
    act, side = total[:width], total[width:]
    block, length = side.shape
    docs = lax.broadcasted_iota(jnp.int32, (SEGS, length), 0)
    member = (docs == segment[...]).astype(jnp.bfloat16)
    group = math.gcd(4, block)
    for start in range(0, block, group):
        outer = jnp.concatenate([(side[i : i + 1] * act).astype(jnp.bfloat16) for i in range(start, start + group)], axis=0)
        sums = lax.dot_general(member, outer, NT, preferred_element_type=jnp.float32)
        out[:, start * width : (start + group) * width] = sums.astype(jnp.bfloat16)


def features(width, segment, keep, received):
    block = keep.shape[0] - width
    return pl.pallas_call(
        functools.partial(features_kernel, width),
        out_shape=jax.ShapeDtypeStruct((SEGS, block * width), jnp.bfloat16),
        in_specs=[VMEM] * (2 + len(received)),
        out_specs=VMEM,
        compiler_params=pltpu.CompilerParams(vmem_limit_bytes=40 * MIB),
        name="features",
    )(segment, keep, *received)


def scores_kernel(parts, members, cores, place, *rest):
    count = members * cores
    blocks, queries = rest[:count], rest[count : count + parts]
    outs, table = rest[count + parts : count + 2 * parts], rest[-1]
    x, h, g, core = place[0], place[1], place[2], place[3]
    for d in range(members):
        for e in range(cores):
            at = holds(g, d, members) * cores + holds(core, e, cores)
            table[pl.ds(pl.multiple_of(at * SEGS, SEGS), SEGS)] = blocks[d * cores + e][...]
    for k in range(parts):
        which = lax.rem(h - x - k + 2 * parts, parts)
        chosen = queries[0][...]
        for d in range(1, parts):
            chosen = jnp.where(which == d, queries[d][...], chosen)
        outs[k][...] = lax.dot_general(chosen, table[...], NT, preferred_element_type=jnp.float32)


def scores(parts, members, cores, place, blocks, queries):
    docs, width = SEGS * len(blocks), blocks[0].shape[1]
    own = queries[0].shape[0]
    return pl.pallas_call(
        functools.partial(scores_kernel, parts, members, cores),
        out_shape=(jax.ShapeDtypeStruct((own, docs), jnp.float32),) * parts,
        in_specs=[SMEM] + [VMEM] * (len(blocks) + parts),
        out_specs=(VMEM,) * parts,
        scratch_shapes=[pltpu.VMEM((docs, width), jnp.bfloat16)],
        compiler_params=pltpu.CompilerParams(vmem_limit_bytes=40 * MIB),
        name="scores",
    )(place, *blocks, *queries)


def sends_to(i, d, size):
    return i ^ d if size & (size - 1) == 0 else (i + d) % size


def holds(i, d, size):
    return i ^ d if size & (size - 1) == 0 else lax.rem(i - d + size, size)


def local(rows_axis, parts, cores, hidden, out_grad, proj_in, proj_out, seg_ids, queries):
    members = rows_axis // parts
    x, q, core = lax.axis_index("tensor"), lax.axis_index("query"), lax.axis_index("dp")
    h, g = q // members, lax.rem(q, members)
    place = jnp.stack([x, h, g, core]).astype(jnp.int32)
    width = proj_in.shape[1]
    around = range(parts)
    asked = [queries]
    for d in range(1, parts):
        pairs = [(a * members + m, (a + d) % parts * members + m) for a in around for m in range(members)]
        asked.append(lax.ppermute(queries, "query", pairs))
    keep, send = project(parts, place, hidden[0], out_grad[0], proj_in.T, proj_out.T)
    received = []
    for d in range(1, parts):
        received.append(lax.ppermute(send[d - 1], "tensor", [(a, (a + d) % parts) for a in around]))
    own = features(width, seg_ids, keep, received)
    blocks = []
    for d in range(members):
        pairs = [(a * members + m, a * members + sends_to(m, d, members)) for a in around for m in range(members)]
        block = lax.ppermute(own, "query", pairs) if d else own
        for e in range(cores):
            pairs = [(c, sends_to(c, e, cores)) for c in range(cores)]
            blocks.append(lax.ppermute(block, "dp", pairs) if e else block)
    partial = scores(parts, members, cores, place, blocks, asked)
    total = None
    for k in range(parts):
        routes = [(a * members + m, b, (b + k) % parts * members + m, a) for a in around for m in range(members) for b in around]
        pairs = [(s * parts + b, t * parts + a) for s, b, t, a in routes if (s, b) != (t, a)]
        arrived = lax.ppermute(partial[k], ("query", "tensor"), pairs)
        at_home = (x == h) & (lax.rem(x + k, parts) == h)
        arrived = jnp.where(at_home, partial[k], arrived) if len(pairs) < len(routes) else arrived
        total = arrived if total is None else total + arrived
    return total.T


def solution(mesh):
    in_specs = (
        P(("query", "dp"), None, "tensor"),
        P(("query", "dp"), None, "tensor"),
        P("tensor", None),
        P("tensor", None),
        P(("query", "dp"), None),
        P(("query", "dp"), "tensor"),
    )
    out_specs = P("tensor", ("query", "dp"))
    step = functools.partial(local, mesh.shape["query"], mesh.shape["tensor"], mesh.shape["dp"])
    return jax.shard_map(step, mesh=mesh, in_specs=in_specs, out_specs=out_specs, check_vma=False)
```

```python
import functools
import math

import jax
import jax.numpy as jnp
from jax import lax
from jax.experimental import pallas as pl
from jax.experimental.pallas import tpu as pltpu
from jax.sharding import PartitionSpec as P

SEGS = 32
MIB = 2**20
NT = (((1,), (1,)), ((), ()))
VMEM = pl.BlockSpec(memory_space=pltpu.VMEM)
SMEM = pl.BlockSpec(memory_space=pltpu.SMEM)
HBM = pl.BlockSpec(memory_space=pltpu.HBM)


def project_kernel(parts, tile, place, hidden, grads, w_in, w_out, keep, send, h_buf, g_buf, wi_buf, wo_buf, out_side, h_sem, g_sem, w_sem):
    length, width = h_buf.shape[0], w_in.shape[0]
    block, steps = width // parts, length // tile

    def rows_of(n):
        return pl.ds(pl.multiple_of(n * tile, tile), tile)

    def copies(n):
        rows = rows_of(n)
        return (
            pltpu.make_async_copy(grads.at[rows], g_buf.at[rows], g_sem.at[n]),
            pltpu.make_async_copy(hidden.at[rows], h_buf.at[rows], h_sem.at[n]),
        )

    weights = (pltpu.make_async_copy(w_out, wo_buf, w_sem.at[0]), pltpu.make_async_copy(w_in, wi_buf, w_sem.at[1]))
    for weight, copy in zip(weights, copies(0)):
        weight.start()
        copy.start()
    for copy in copies(1) if steps > 1 else ():
        copy.start()
    for weight in weights:
        weight.wait()

    def step(n, carry):
        rows = rows_of(n)
        for copy in copies(n):
            copy.wait()

        @pl.when(n + 2 < steps)
        def _():
            for copy in copies(n + 2):
                copy.start()

        act = lax.dot_general(h_buf[rows], wi_buf[...], NT, preferred_element_type=jnp.float32)
        side = lax.dot_general(g_buf[rows], wo_buf[...], NT, preferred_element_type=jnp.float32)
        both = jnp.concatenate([act, side], axis=1).T
        keep[:width, rows] = both[:width]
        for d in range(1, parts):
            send[d - 1, :width, rows] = both[:width].astype(jnp.bfloat16)
        out_side[:, rows] = both[width:]
        return carry

    lax.fori_loop(0, steps, step, 0)
    keep[width:] = out_side[pl.ds(pl.multiple_of(place[0] * block, block), block)]
    for d in range(1, parts):
        there = lax.rem(place[0] + d, parts)
        send[d - 1, width:] = out_side[pl.ds(pl.multiple_of(there * block, block), block)].astype(jnp.bfloat16)


def project(parts, place, hidden, grads, w_in, w_out):
    (length, units), features, width = hidden.shape, grads.shape[1], w_in.shape[0]
    tile = math.gcd(length, 256)
    rows, steps = width + width // parts, length // tile
    return pl.pallas_call(
        functools.partial(project_kernel, parts, tile),
        out_shape=(
            jax.ShapeDtypeStruct((rows, length), jnp.float32),
            jax.ShapeDtypeStruct((max(parts - 1, 1), rows, length), jnp.bfloat16),
        ),
        in_specs=[SMEM, HBM, HBM, HBM, HBM],
        out_specs=(VMEM, VMEM),
        scratch_shapes=[
            pltpu.VMEM((length, units), jnp.bfloat16),
            pltpu.VMEM((length, features), jnp.bfloat16),
            pltpu.VMEM((width, units), jnp.bfloat16),
            pltpu.VMEM((width, features), jnp.bfloat16),
            pltpu.VMEM((width, length), jnp.float32),
            pltpu.SemaphoreType.DMA((steps,)),
            pltpu.SemaphoreType.DMA((steps,)),
            pltpu.SemaphoreType.DMA((2,)),
        ],
        compiler_params=pltpu.CompilerParams(vmem_limit_bytes=40 * MIB),
        name="project",
    )(place, *(pltpu.with_memory_space_constraint(a, pltpu.HBM) for a in (hidden, grads, w_in, w_out)))


def features_kernel(width, segment, keep, *rest):
    received, out = rest[:-1], rest[-1]
    total = keep[...]
    for other in received:
        total = total + other[...].astype(jnp.float32)
    act, side = total[:width], total[width:]
    block, length = side.shape
    docs = lax.broadcasted_iota(jnp.int32, (SEGS, length), 0)
    member = (docs == segment[...]).astype(jnp.bfloat16)
    group = math.gcd(4, block)
    for start in range(0, block, group):
        outer = jnp.concatenate([(side[i : i + 1] * act).astype(jnp.bfloat16) for i in range(start, start + group)], axis=0)
        sums = lax.dot_general(member, outer, NT, preferred_element_type=jnp.float32)
        out[:, start * width : (start + group) * width] = sums.astype(jnp.bfloat16)


def features(width, segment, keep, received):
    block = keep.shape[0] - width
    return pl.pallas_call(
        functools.partial(features_kernel, width),
        out_shape=jax.ShapeDtypeStruct((SEGS, block * width), jnp.bfloat16),
        in_specs=[VMEM] * (2 + len(received)),
        out_specs=VMEM,
        compiler_params=pltpu.CompilerParams(vmem_limit_bytes=40 * MIB),
        name="features",
    )(segment, keep, *received)


def scores_kernel(parts, members, cores, place, *rest):
    count = members * cores
    blocks, queries = rest[:count], rest[count : count + parts]
    outs, table = rest[count + parts : count + 2 * parts], rest[-1]
    x, h, g, core = place[0], place[1], place[2], place[3]
    for d in range(members):
        for e in range(cores):
            at = holds(g, d, members) * cores + holds(core, e, cores)
            table[pl.ds(pl.multiple_of(at * SEGS, SEGS), SEGS)] = blocks[d * cores + e][...]
    for k in range(parts):
        which = lax.rem(h - x - k + 2 * parts, parts)
        chosen = queries[0][...]
        for d in range(1, parts):
            chosen = jnp.where(which == d, queries[d][...], chosen)
        outs[k][...] = lax.dot_general(chosen, table[...], NT, preferred_element_type=jnp.float32)


def scores(parts, members, cores, place, blocks, queries):
    docs, width = SEGS * len(blocks), blocks[0].shape[1]
    own = queries[0].shape[0]
    return pl.pallas_call(
        functools.partial(scores_kernel, parts, members, cores),
        out_shape=(jax.ShapeDtypeStruct((own, docs), jnp.float32),) * parts,
        in_specs=[SMEM] + [VMEM] * (len(blocks) + parts),
        out_specs=(VMEM,) * parts,
        scratch_shapes=[pltpu.VMEM((docs, width), jnp.bfloat16)],
        compiler_params=pltpu.CompilerParams(vmem_limit_bytes=40 * MIB),
        name="scores",
    )(place, *blocks, *queries)


def sends_to(i, d, size):
    return i ^ d if size & (size - 1) == 0 else (i + d) % size


def holds(i, d, size):
    return i ^ d if size & (size - 1) == 0 else lax.rem(i - d + size, size)


def local(rows_axis, parts, cores, hidden, out_grad, proj_in, proj_out, seg_ids, queries):
    members = rows_axis // parts
    x, q, core = lax.axis_index("tensor"), lax.axis_index("query"), lax.axis_index("dp")
    h, g = q // members, lax.rem(q, members)
    place = jnp.stack([x, h, g, core]).astype(jnp.int32)
    width = proj_in.shape[1]
    around = range(parts)
    asked = [queries]
    for d in range(1, parts):
        pairs = [(a * members + m, (a + d) % parts * members + m) for a in around for m in range(members)]
        asked.append(lax.ppermute(queries, "query", pairs))
    keep, send = project(parts, place, hidden[0], out_grad[0], proj_in.T, proj_out.T)
    received = []
    for d in range(1, parts):
        received.append(lax.ppermute(send[d - 1], "tensor", [(a, (a + d) % parts) for a in around]))
    own = features(width, seg_ids, keep, received)
    blocks = []
    for d in range(members):
        pairs = [(a * members + m, a * members + sends_to(m, d, members)) for a in around for m in range(members)]
        block = lax.ppermute(own, "query", pairs) if d else own
        for e in range(cores):
            pairs = [(c, sends_to(c, e, cores)) for c in range(cores)]
            blocks.append(lax.ppermute(block, "dp", pairs) if e else block)
    partial = scores(parts, members, cores, place, blocks, asked)
    total = None
    for k in reversed(range(parts)):
        routes = [(a * members + m, b, (b + k) % parts * members + m, a) for a in around for m in range(members) for b in around]
        pairs = [(s * parts + b, t * parts + a) for s, b, t, a in routes if (s, b) != (t, a)]
        arrived = lax.ppermute(partial[k], ("query", "tensor"), pairs)
        at_home = (x == h) & (lax.rem(x + k, parts) == h)
        arrived = jnp.where(at_home, partial[k], arrived) if len(pairs) < len(routes) else arrived
        total = arrived if total is None else total + arrived
    return total.T


def solution(mesh):
    in_specs = (
        P(("query", "dp"), None, "tensor"),
        P(("query", "dp"), None, "tensor"),
        P("tensor", None),
        P("tensor", None),
        P(("query", "dp"), None),
        P(("query", "dp"), "tensor"),
    )
    out_specs = P("tensor", ("query", "dp"))
    body = functools.partial(local, mesh.shape["query"], mesh.shape["tensor"], mesh.shape["dp"])

    return jax.shard_map(body, mesh=mesh, in_specs=in_specs, out_specs=out_specs, check_vma=False)
```

```python
import functools
import math

import jax
import jax.numpy as jnp
from jax import lax
from jax.experimental import pallas as pl
from jax.experimental.pallas import tpu as pltpu
from jax.sharding import PartitionSpec as P

SEGS = 32
MIB = 2**20
NT = (((1,), (1,)), ((), ()))
VMEM = pl.BlockSpec(memory_space=pltpu.VMEM)
SMEM = pl.BlockSpec(memory_space=pltpu.SMEM)
HBM = pl.BlockSpec(memory_space=pltpu.HBM)


def project_kernel(parts, tile, place, hidden, grads, w_in, w_out, keep, send, h_buf, g_buf, wi_buf, wo_buf, out_side, h_sem, g_sem, w_sem):
    length, width = h_buf.shape[0], w_in.shape[0]
    block, steps = width // parts, length // tile

    def rows_of(n):
        return pl.ds(pl.multiple_of(n * tile, tile), tile)

    def copies(n):
        rows = rows_of(n)
        return (
            pltpu.make_async_copy(grads.at[rows], g_buf.at[rows], g_sem.at[n]),
            pltpu.make_async_copy(hidden.at[rows], h_buf.at[rows], h_sem.at[n]),
        )

    weights = (pltpu.make_async_copy(w_out, wo_buf, w_sem.at[0]), pltpu.make_async_copy(w_in, wi_buf, w_sem.at[1]))
    for weight, copy in zip(weights, copies(0)):
        weight.start()
        copy.start()
    for copy in copies(1) if steps > 1 else ():
        copy.start()
    for weight in weights:
        weight.wait()

    def step(n, carry):
        rows = rows_of(n)
        for copy in copies(n):
            copy.wait()

        @pl.when(n + 2 < steps)
        def _():
            for copy in copies(n + 2):
                copy.start()

        act = lax.dot_general(h_buf[rows], wi_buf[...], NT, preferred_element_type=jnp.float32)
        side = lax.dot_general(g_buf[rows], wo_buf[...], NT, preferred_element_type=jnp.float32)
        both = jnp.concatenate([act, side], axis=1).T
        keep[:width, rows] = both[:width]
        for d in range(1, parts):
            send[d - 1, :width, rows] = both[:width].astype(jnp.bfloat16)
        out_side[:, rows] = both[width:]
        return carry

    lax.fori_loop(0, steps, step, 0)
    keep[width:] = out_side[pl.ds(pl.multiple_of(place[0] * block, block), block)]
    for d in range(1, parts):
        there = lax.rem(place[0] + d, parts)
        send[d - 1, width:] = out_side[pl.ds(pl.multiple_of(there * block, block), block)].astype(jnp.bfloat16)


def project(parts, place, hidden, grads, w_in, w_out):
    (length, units), features, width = hidden.shape, grads.shape[1], w_in.shape[0]
    tile = math.gcd(length, 256)
    rows, steps = width + width // parts, length // tile
    return pl.pallas_call(
        functools.partial(project_kernel, parts, tile),
        out_shape=(
            jax.ShapeDtypeStruct((rows, length), jnp.float32),
            jax.ShapeDtypeStruct((max(parts - 1, 1), rows, length), jnp.bfloat16),
        ),
        in_specs=[SMEM, HBM, HBM, HBM, HBM],
        out_specs=(VMEM, VMEM),
        scratch_shapes=[
            pltpu.VMEM((length, units), jnp.bfloat16),
            pltpu.VMEM((length, features), jnp.bfloat16),
            pltpu.VMEM((width, units), jnp.bfloat16),
            pltpu.VMEM((width, features), jnp.bfloat16),
            pltpu.VMEM((width, length), jnp.float32),
            pltpu.SemaphoreType.DMA((steps,)),
            pltpu.SemaphoreType.DMA((steps,)),
            pltpu.SemaphoreType.DMA((2,)),
        ],
        compiler_params=pltpu.CompilerParams(vmem_limit_bytes=40 * MIB),
        name="project",
    )(place, *(pltpu.with_memory_space_constraint(a, pltpu.HBM) for a in (hidden, grads, w_in, w_out)))


def features_kernel(width, segment, keep, *rest):
    received, out = rest[:-1], rest[-1]
    total = keep[...]
    for other in received:
        total = total + other[...].astype(jnp.float32)
    act, side = total[:width], total[width:]
    block, length = side.shape
    docs = lax.broadcasted_iota(jnp.int32, (SEGS, length), 0)
    member = (docs == segment[...]).astype(jnp.bfloat16)
    group = math.gcd(4, block)
    for start in range(0, block, group):
        outer = jnp.concatenate([(side[i : i + 1] * act).astype(jnp.bfloat16) for i in range(start, start + group)], axis=0)
        sums = lax.dot_general(member, outer, NT, preferred_element_type=jnp.float32)
        out[:, start * width : (start + group) * width] = sums.astype(jnp.bfloat16)


def features(width, segment, keep, received):
    block = keep.shape[0] - width
    return pl.pallas_call(
        functools.partial(features_kernel, width),
        out_shape=jax.ShapeDtypeStruct((SEGS, block * width), jnp.bfloat16),
        in_specs=[VMEM] * (2 + len(received)),
        out_specs=VMEM,
        compiler_params=pltpu.CompilerParams(vmem_limit_bytes=40 * MIB),
        name="features",
    )(segment, keep, *received)


def scores_kernel(parts, near, cores, place, *rest):
    count = near * cores
    blocks, rest = rest[:count], rest[count:]
    asked = len(rest) // 2 - 1
    queries, outs, docs, rows = rest[:asked], rest[asked : 2 * asked], rest[-2], rest[-1]
    x, h, b, core = place[0], place[1], place[2], place[3]
    far, own = asked // parts, queries[0].shape[0]
    for d in range(parts):
        k = lax.rem(h - x - d + 2 * parts, parts)
        for s in range(far):
            rows[pl.ds(pl.multiple_of((k * far + s) * own, own), own)] = queries[d * far + s][...]
    for d in range(near):
        for e in range(cores):
            at = holds(b, d, near) * cores + holds(core, e, cores)
            docs[pl.ds(pl.multiple_of(at * SEGS, SEGS), SEGS)] = blocks[d * cores + e][...]
    table = lax.dot_general(rows[...], docs[...], NT, preferred_element_type=jnp.float32)
    for n, out in enumerate(outs):
        out[...] = table[n * own : (n + 1) * own]


def scores(parts, near, cores, place, blocks, queries):
    docs, width = SEGS * len(blocks), blocks[0].shape[1]
    own = queries[0].shape[0]
    return pl.pallas_call(
        functools.partial(scores_kernel, parts, near, cores),
        out_shape=(jax.ShapeDtypeStruct((own, docs), jnp.float32),) * len(queries),
        in_specs=[SMEM] + [VMEM] * (len(blocks) + len(queries)),
        out_specs=(VMEM,) * len(queries),
        scratch_shapes=[pltpu.VMEM((docs, width), jnp.bfloat16), pltpu.VMEM((own * len(queries), width), jnp.bfloat16)],
        compiler_params=pltpu.CompilerParams(vmem_limit_bytes=40 * MIB),
        name="scores",
    )(place, *blocks, *queries)


def sends_to(i, d, size):
    return i ^ d if size & (size - 1) == 0 else (i + d) % size


def holds(i, d, size):
    return i ^ d if size & (size - 1) == 0 else (i - d) % size


def local(rows_axis, parts, cores, hidden, out_grad, proj_in, proj_out, seg_ids, queries):
    members = rows_axis // parts
    near = max(n for n in range(1, math.isqrt(members) + 1) if members % n == 0)
    far = members // near
    x, q, core = lax.axis_index("tensor"), lax.axis_index("query"), lax.axis_index("dp")
    h, a, b = q // members, lax.rem(q, members) // near, lax.rem(q, near)
    place = jnp.stack([x, h, b, core]).astype(jnp.int32)
    width = proj_in.shape[1]
    every = [(i, j, m) for i in range(parts) for j in range(far) for m in range(near)]

    def index(i, j, m):
        return (i * far + j) * near + m

    asked = {(0, 0): queries}
    for d in range(1, parts):
        asked[d, 0] = lax.ppermute(queries, "query", [(index(i, j, m), index((i + d) % parts, j, m)) for i, j, m in every])
    for d in range(parts):
        for s in range(1, far):
            asked[d, s] = lax.ppermute(asked[d, 0], "query", [(index(i, j, m), index(i, sends_to(j, s, far), m)) for i, j, m in every])
    keep, send = project(parts, place, hidden[0], out_grad[0], proj_in.T, proj_out.T)
    received = []
    for d in range(1, parts):
        received.append(lax.ppermute(send[d - 1], "tensor", [(i, (i + d) % parts) for i in range(parts)]))
    own = features(width, seg_ids, keep, received)
    blocks = []
    for d in range(near):
        pairs = [(index(i, j, m), index(i, j, sends_to(m, d, near))) for i, j, m in every]
        block = lax.ppermute(own, "query", pairs) if d else own
        for e in range(cores):
            blocks.append(lax.ppermute(block, "dp", [(c, sends_to(c, e, cores)) for c in range(cores)]) if e else block)
    slots = [(k, s) for k in range(parts) for s in range(far)]
    partial = dict(zip(slots, scores(parts, near, cores, place, blocks, [asked[slot] for slot in slots])))
    totals = []
    for s in range(far):
        total = None
        for k in range(parts):
            routes = [
                (index(i, j, m) * parts + t, index((t + k) % parts, int(holds(j, s, far)), m) * parts + i)
                for i, j, m in every
                for t in range(parts)
            ]
            pairs = [(source, target) for source, target in routes if source != target]
            arrived = lax.ppermute(partial[k, s], ("query", "tensor"), pairs)
            if len(pairs) < len(routes):
                arrived = jnp.where((x == h) & (lax.rem(x + k, parts) == h), partial[k, s], arrived)
            total = arrived if total is None else total + arrived
        totals.append(total)
    found = []
    for j in range(far):
        block = totals[0]
        for s in range(1, far):
            block = jnp.where(sends_to(a, s, far) == j, totals[s], block)
        found.append(block)
    return jnp.concatenate(found, axis=1).T


def solution(mesh):
    in_specs = (
        P(("query", "dp"), None, "tensor"),
        P(("query", "dp"), None, "tensor"),
        P("tensor", None),
        P("tensor", None),
        P(("query", "dp"), None),
        P(("query", "dp"), "tensor"),
    )
    out_specs = P("tensor", ("query", "dp"))
    body = functools.partial(local, mesh.shape["query"], mesh.shape["tensor"], mesh.shape["dp"])

    return jax.shard_map(body, mesh=mesh, in_specs=in_specs, out_specs=out_specs, check_vma=False)
```
